32 devices in a mesh: pair: 8 (over z, y), aux: 4 (over x, core).
Axes of the slice: x: 2, y: 2, z: 4, core: 2. Of those that a mesh axis runs over, the one named last changes fastest.
Arguments:
- amplitudes: float32 [896, 8, 896], P('aux', 'pair'), may hold values from -6 to 6
- fitting: float32 [4, 896, 896], P('aux', 'pair'), may hold values from -0.09375 to 0.09375
Outputs:
- ladder: float32 [896, 8, 896], P('aux', 'pair')
The draws below stay inside these ranges and needn't reach their ends.
All inputs are finite; a program needn't handle non-finite values.
Results may differ from the reference program's by a relative error of at most 0.0001.
Values sent between devices are 32-bit elements; how exact they have to be, the bound alone decides.
A program may use at most 64 MiB of HBM per device.

```python
import jax
import jax.numpy as jnp
from jax import lax

V = 896
NPAIRS = 8
NFIT = 4


def level_of(own_key, extent, split, least, largest):
    gain, own = 1.0, jax.random.fold_in(own_key, 6)
    for position, parts in split:
        draws = jnp.exp(jax.random.uniform(jax.random.fold_in(own, position), (parts,), jnp.float32, least / len(split), largest / len(split)))
        gain = gain * jnp.repeat(draws, extent[position] // parts).reshape([-1 if axis == position else 1 for axis in range(len(extent))])
    return gain


def gaussian(stream_key, extent, width, reach, pieces=(), dtype=jnp.bfloat16):
    entries = width * jax.random.normal(stream_key, extent, jnp.float32)
    if pieces:
        entries = entries * level_of(stream_key, extent, pieces, -0.22, 0.18)
    return jnp.clip(entries, -reach, reach).astype(dtype)


def setup_inputs(seed: int = 0) -> dict:
    splits = jax.random.split(jax.random.key(seed), 3)
    amplitudes = gaussian(splits[0], (V, NPAIRS, V), 1.0, 6.0, ((0, 4), (1, 8)), jnp.float32)
    fitting = gaussian(splits[1], (NFIT, V, V), (V * 4) ** -0.5, 0.09375, ((0, 4), (1, 8)), jnp.float32)
    return dict(amplitudes=amplitudes, fitting=fitting)


def reference(amplitudes, fitting):
    flat = amplitudes.reshape(V * NPAIRS, V)

    def step(total, matrix):
        half = jnp.dot(flat, matrix.T, precision=lax.Precision.HIGHEST, preferred_element_type=jnp.float32)
        half = half.reshape(V, NPAIRS * V)
        return total + jnp.dot(matrix, half, precision=lax.Precision.HIGHEST, preferred_element_type=jnp.float32), None

    total, _ = lax.scan(step, jnp.zeros((V, NPAIRS * V), jnp.float32), fitting)
    return total.reshape(V, NPAIRS, V)
```

```python
import functools

import jax
import jax.numpy as jnp
from jax import lax
from jax.experimental import pallas as pl
from jax.experimental.pallas import tpu as pltpu
from jax.sharding import PartitionSpec as P

MESH = pl.DeviceIdType.MESH
F32, BF16 = jnp.float32, jnp.bfloat16
NT = (((1,), (1,)), ((), ()))


def ring_order(n):
    depth = 4 if n % 4 == 0 and n > 4 else 2
    width = n // depth
    if n % 2 or width < 2:
        return list(range(n))
    walk = []
    for z in range(depth):
        ys = range(1, width) if z % 2 == 0 else range(width - 1, 0, -1)
        walk += [z * width + y for y in ys]
    return walk + [z * width for z in range(depth - 1, -1, -1)]


def lookup(table, key):
    return sum(jnp.where(key == k, v, 0) for k, v in enumerate(table))


def split(v):
    high = v.astype(BF16).astype(F32)
    return high, v - high


def kernel(
    n, chips, parts, cut,
    t_in, b_in, out,
    t_all, b_all, t_high, t_low, b_high, b_low, g_all,
    mate_out, mate_in, sum_out, sum_in,
    local_sem, right_send, right_recv, left_send, left_recv,
    tx_send, tx_recv, tm_send, tm_recv, pm_send, pm_recv, px_send, px_recv,
):
    width = t_all.shape[1]
    rows_t, rows_b = t_in.shape[0], b_in.shape[0]
    piece = rows_t // parts
    reach = n // 2
    order = ring_order(n)
    where = [order.index(k) for k in range(n)]
    pair, aux = lax.axis_index("pair"), lax.axis_index("aux")
    chip, core = aux // 2, aux % 2
    mate = chip * 2 + (1 - core)
    spot = lookup(where, pair)

    def at(step):
        return lookup(order, lax.rem(spot + step + n, n))

    right, left = at(1), at(-1)

    def chip_at(step):
        return lax.rem(chip + step + chips, chips)

    barrier = pltpu.get_barrier_semaphore()
    greet = [(right, aux), (left, aux), (pair, mate)]
    greet += [(pair, chip_at(e) * 2 + core) for e in range(1, chips)]
    for who in greet:
        pl.semaphore_signal(barrier, inc=1, device_id=who, device_id_type=MESH)
    pl.semaphore_wait(barrier, len(greet))

    bounds = [(0, cut), (cut, rows_b - cut)]

    def b_rows(block, h):
        start, size = bounds[h]
        return pl.ds(pl.multiple_of(block * rows_b + start, 8), size)

    def t_rows(owner, s):
        return pl.ds(pl.multiple_of(owner * rows_t + s * piece, 8), piece)

    def hop(d, h, to_right):
        step = (1 - d) if to_right else (d - 1)
        block = at(step)
        rows = b_rows(block, h)
        start, size = bounds[h]
        src = b_in.at[pl.ds(start, size)] if d == 1 else b_all.at[rows]
        send, recv = (right_send, right_recv) if to_right else (left_send, left_recv)
        return pltpu.make_async_remote_copy(
            src_ref=src,
            dst_ref=b_all.at[rows],
            send_sem=send.at[d - 1, h],
            recv_sem=recv.at[d - 1, h],
            device_id=(right if to_right else left, aux),
            device_id_type=MESH,
        )

    def arrive(d, h, from_left):
        block = at(-d if from_left else d)
        rows = b_rows(block, h)
        send, recv = (right_send, right_recv) if from_left else (left_send, left_recv)
        pltpu.make_async_remote_copy(
            src_ref=b_all.at[rows],
            dst_ref=b_all.at[rows],
            send_sem=send.at[d - 1, h],
            recv_sem=recv.at[d - 1, h],
            device_id=(left if from_left else right, aux),
            device_id_type=MESH,
        ).wait_recv()

    def carried(d, h, to_right):
        return d < reach or (h == 0) == to_right

    def t_cross(e, s):
        return pltpu.make_async_remote_copy(
            src_ref=t_in.at[pl.ds(s * piece, piece)],
            dst_ref=t_all.at[t_rows(aux, s)],
            send_sem=tx_send.at[e - 1, s],
            recv_sem=tx_recv.at[e - 1, s],
            device_id=(pair, chip_at(e) * 2 + core),
            device_id_type=MESH,
        )

    def t_mate(e, s):
        rows = t_rows(chip_at(-e) * 2 + core, s)
        return pltpu.make_async_remote_copy(
            src_ref=t_in.at[pl.ds(s * piece, piece)] if e == 0 else t_all.at[rows],
            dst_ref=t_all.at[rows],
            send_sem=tm_send.at[e, s],
            recv_sem=tm_recv.at[e, s],
            device_id=(pair, mate),
            device_id_type=MESH,
        )

    def landed(ref, rows, send, recv):
        pltpu.make_async_remote_copy(
            src_ref=ref.at[rows], dst_ref=ref.at[rows], send_sem=send, recv_sem=recv,
            device_id=(pair, mate), device_id_type=MESH,
        ).wait_recv()

    started = []

    def go(copy):
        copy.start()
        started.append(copy)

    for h in range(2):
        for to_right in (True, False):
            if carried(1, h, to_right):
                go(hop(1, h, to_right))
    for s in range(parts):
        for e in range(1, chips):
            go(t_cross(e, s))
    for s in range(parts):
        go(t_mate(0, s))
    own_b = pltpu.make_async_copy(
        b_in, b_all.at[pl.ds(pl.multiple_of(pair * rows_b, 8), rows_b)], local_sem.at[0]
    )
    own_t = pltpu.make_async_copy(
        t_in, t_all.at[pl.ds(pl.multiple_of(aux * rows_t, 8), rows_t)], local_sem.at[1]
    )
    own_b.start()
    own_t.start()
    own_b.wait()
    own_t.wait()

    def relay(d):
        for h in range(2):
            for from_left in (True, False):
                if carried(d, h, from_left):
                    arrive(d, h, from_left)
                    if d < reach and carried(d + 1, h, from_left):
                        go(hop(d + 1, h, from_left))

    def t_relay(s):
        for e in range(1, chips):
            landed(
                t_all, t_rows(chip_at(-e) * 2 + core, s),
                tx_send.at[e - 1, s], tx_recv.at[e - 1, s],
            )
            go(t_mate(e, s))

    def first_product(block):
        rows = pl.ds(pl.multiple_of(block * rows_b, 8), rows_b)
        high, low = split(b_all[rows, :])
        if rows_b % 16 == 0:
            b_high[pl.ds(pl.multiple_of(block * rows_b, 16), rows_b), :] = high.astype(BF16)
            b_low[pl.ds(pl.multiple_of(block * rows_b, 16), rows_b), :] = low.astype(BF16)
        both = jnp.concatenate([high, low], axis=0).astype(BF16)
        main = jnp.dot(both, t_high[...], preferred_element_type=F32)
        rest = jnp.dot(high.astype(BF16), t_low[...], preferred_element_type=F32)
        g_all[rows, :] = main[:rows_b] + (main[rows_b:] + rest)

    early = max(1, reach - 2)
    for d in range(1, early + 1):
        relay(d)
        if d <= parts:
            t_relay(d - 1)
    for s in range(min(early, parts), parts):
        t_relay(s)
    for e in range(chips):
        for s in range(parts):
            landed(
                t_all, t_rows(chip_at(-e) * 2 + (1 - core), s),
                tm_send.at[e, s], tm_recv.at[e, s],
            )

    @pl.loop(0, width // 128)
    def _(i):
        rows = pl.ds(pl.multiple_of(i * 128, 128), 128)
        high, low = split(t_all[rows, :])
        t_high[rows, :] = high.astype(BF16)
        t_low[rows, :] = low.astype(BF16)

    @pl.loop(-(early - 1), early)
    def _(i):
        first_product(at(i))

    def both_sides(d):
        @pl.loop(0, 2)
        def _(i):
            first_product(at((2 * i - 1) * d))

    for d in range(early + 1, reach):
        relay(d)
        both_sides(d - 1)
    if reach > 1:
        both_sides(reach - 1)
    relay(reach)
    first_product(at(reach))

    if rows_b % 16:
        @pl.loop(0, width // 128)
        def _(i):
            rows = pl.ds(pl.multiple_of(i * 128, 128), 128)
            high, low = split(b_all[rows, :])
            b_high[rows, :] = high.astype(BF16)
            b_low[rows, :] = low.astype(BF16)

    def second_product(owner, s):
        high, low = split(g_all[t_rows(owner, s), :])
        both = jnp.concatenate([high, low], axis=0).astype(BF16)
        main = lax.dot_general(both, b_high[...], NT, preferred_element_type=F32)
        rest = lax.dot_general(high.astype(BF16), b_low[...], NT, preferred_element_type=F32)
        return main[:piece] + (main[piece:] + rest)

    def p_mate(e, s):
        return pltpu.make_async_remote_copy(
            src_ref=mate_out.at[e, s], dst_ref=mate_in.at[e, s],
            send_sem=pm_send.at[e, s], recv_sem=pm_recv.at[e, s],
            device_id=(pair, mate), device_id_type=MESH,
        )

    def p_cross(e, s):
        return pltpu.make_async_remote_copy(
            src_ref=sum_out.at[e - 1, s], dst_ref=sum_in.at[e - 1, s],
            send_sem=px_send.at[e - 1, s], recv_sem=px_recv.at[e - 1, s],
            device_id=(pair, chip_at(e) * 2 + core), device_id_type=MESH,
        )

    def chip_sum(e, s):
        mate_out[e, s] = second_product(chip_at(e) * 2 + (1 - core), s)
        p_mate(e, s).start()
        mine = second_product(chip_at(e) * 2 + core, s)
        p_mate(e, s).wait_recv()
        return mine + mate_in[e, s]

    @pl.loop(0, (chips - 1) * parts)
    def _(i):
        e, s = i // parts + 1, i % parts
        sum_out[e - 1, s] = chip_sum(e, s)
        p_cross(e, s).start()

    @pl.loop(0, parts)
    def _(s):
        out[pl.ds(pl.multiple_of(s * piece, 8), piece), :] = chip_sum(0, s)

    for s in range(parts):
        rows = pl.ds(s * piece, piece)
        for e in range(1, chips):
            p_cross(e, s).wait_recv()
            out[rows, :] += sum_in[e - 1, s]

    for copy in started:
        copy.wait_send()
    for e in range(chips):
        for s in range(parts):
            p_mate(e, s).wait_send()
            if e:
                p_cross(e, s).wait_send()


def per_device(n, n_aux, amplitudes, fitting):
    rows_t, pair_dev, width = amplitudes.shape
    count_fit, rows_b, _ = fitting.shape
    assert pair_dev == 1 and count_fit == 1
    chips = n_aux // 2
    parts = 2 if rows_t % 16 == 0 else 1
    piece = rows_t // parts
    cut = rows_b // 16 * 8
    reach = n // 2
    dma = pltpu.SemaphoreType.DMA
    whole_f32 = pltpu.VMEM((width, width), F32)
    whole_bf16 = pltpu.VMEM((width, width), BF16)
    blocks = lambda k: pltpu.VMEM((k, parts, piece, width), F32)
    result = pl.pallas_call(
        functools.partial(kernel, n, chips, parts, cut),
        out_shape=jax.ShapeDtypeStruct((rows_t, width), F32),
        in_specs=[pl.BlockSpec(memory_space=pl.ANY)] * 2,
        out_specs=pl.BlockSpec(memory_space=pltpu.VMEM),
        scratch_shapes=[
            whole_f32, whole_f32, whole_bf16, whole_bf16, whole_bf16, whole_bf16, whole_f32,
            blocks(chips), blocks(chips), blocks(chips - 1), blocks(chips - 1),
            dma((2,)),
            dma((reach, 2)), dma((reach, 2)), dma((reach, 2)), dma((reach, 2)),
            dma((chips - 1, parts)), dma((chips - 1, parts)),
            dma((chips, parts)), dma((chips, parts)),
            dma((chips, parts)), dma((chips, parts)),
            dma((chips - 1, parts)), dma((chips - 1, parts)),
        ],
        compiler_params=pltpu.CompilerParams(
            collective_id=0, has_side_effects=True, vmem_limit_bytes=60 << 20
        ),
    )(amplitudes.reshape(rows_t, width), fitting.reshape(rows_b, width))
    return result.reshape(rows_t, pair_dev, width)


def solution(mesh):
    spec = P("aux", "pair", None)
    return jax.shard_map(
        functools.partial(per_device, mesh.shape["pair"], mesh.shape["aux"]),
        mesh=mesh, in_specs=(spec, spec), out_specs=spec, check_vma=False,
    )
```

```python
import functools

import jax
import jax.numpy as jnp
from jax import lax
from jax.experimental import pallas as pl
from jax.experimental.pallas import tpu as pltpu
from jax.sharding import PartitionSpec as P

MESH = pl.DeviceIdType.MESH
CUTS, PARTS = 4, 4
F32, BF16 = jnp.float32, jnp.bfloat16
NT = (((1,), (1,)), ((), ()))


def ring_order(n):
    depth = 4 if n % 4 == 0 and n > 4 else 2
    width = n // depth
    if n % 2 or width < 2:
        return list(range(n))
    walk = []
    for z in range(depth):
        ys = range(1, width) if z % 2 == 0 else range(width - 1, 0, -1)
        walk += [z * width + y for y in ys]
    return walk + [z * width for z in range(depth - 1, -1, -1)]


def lookup(table, key):
    return sum(jnp.where(key == k, v, 0) for k, v in enumerate(table))


def split(v):
    high = v.astype(BF16).astype(F32)
    return high, v - high


def kernel(
    n, chips, parts, cuts,
    t_in, b_in, out,
    t_all, b_all, t_high, t_low, b_high, b_low, g_all,
    mate_out, mate_in, sum_out, sum_in, kept,
    local_sem, right_send, right_recv, left_send, left_recv,
    tx_send, tx_recv, tm_send, tm_recv, pm_send, pm_recv, px_send, px_recv,
):
    rows_b, width = b_in.shape
    lanes = t_in.shape[1]
    tiles = width // lanes
    rows_t = t_in.shape[0] // tiles
    piece = rows_t // parts
    reach = n // 2
    order = ring_order(n)
    where = [order.index(k) for k in range(n)]
    pair, aux = lax.axis_index("pair"), lax.axis_index("aux")
    chip, core = aux // 2, aux % 2
    mate = chip * 2 + (1 - core)
    spot = lookup(where, pair)

    def at(step):
        return lookup(order, lax.rem(spot + step + n, n))

    right, left = at(1), at(-1)

    def chip_at(step):
        return lax.rem(chip + step + chips, chips)

    barrier = pltpu.get_barrier_semaphore()
    greet = [(right, aux), (left, aux), (pair, mate)]
    greet += [(pair, chip_at(e) * 2 + core) for e in range(1, chips)]
    for who in greet:
        pl.semaphore_signal(barrier, inc=1, device_id=who, device_id_type=MESH)
    pl.semaphore_wait(barrier, len(greet))

    edges = [rows_b // 8 * k // cuts * 8 for k in range(cuts)] + [rows_b]
    bounds = [(a, b - a) for a, b in zip(edges, edges[1:])]

    def b_rows(block, h):
        start, size = bounds[h]
        return pl.ds(pl.multiple_of(block * rows_b + start, 8), size)

    def g_rows(owner, s):
        return pl.ds(pl.multiple_of(owner * rows_t + s * piece, 8), piece)

    def t_rows(owner, s):
        start = (owner * rows_t + s * piece) * tiles
        return pl.ds(pl.multiple_of(start, 8), piece * tiles)

    def t_own(s):
        return pl.ds(s * piece * tiles, piece * tiles)

    def hop(d, h, to_right):
        step = (1 - d) if to_right else (d - 1)
        block = at(step)
        rows = b_rows(block, h)
        start, size = bounds[h]
        src = b_in.at[pl.ds(start, size)] if d == 1 else b_all.at[rows]
        send, recv = (right_send, right_recv) if to_right else (left_send, left_recv)
        return pltpu.make_async_remote_copy(
            src_ref=src,
            dst_ref=b_all.at[rows],
            send_sem=send.at[d - 1, h],
            recv_sem=recv.at[d - 1, h],
            device_id=(right if to_right else left, aux),
            device_id_type=MESH,
        )

    def arrive(d, h, from_left):
        block = at(-d if from_left else d)
        rows = b_rows(block, h)
        send, recv = (right_send, right_recv) if from_left else (left_send, left_recv)
        pltpu.make_async_remote_copy(
            src_ref=b_all.at[rows],
            dst_ref=b_all.at[rows],
            send_sem=send.at[d - 1, h],
            recv_sem=recv.at[d - 1, h],
            device_id=(left if from_left else right, aux),
            device_id_type=MESH,
        ).wait_recv()

    def carried(d, h, to_right):
        return d < reach or (h < cuts // 2) == to_right

    def t_cross(e, s):
        return pltpu.make_async_remote_copy(
            src_ref=t_in.at[t_own(s)],
            dst_ref=t_all.at[t_rows(aux, s)],
            send_sem=tx_send.at[e - 1, s],
            recv_sem=tx_recv.at[e - 1, s],
            device_id=(pair, chip_at(e) * 2 + core),
            device_id_type=MESH,
        )

    def t_mate(e, s):
        rows = t_rows(chip_at(-e) * 2 + core, s)
        return pltpu.make_async_remote_copy(
            src_ref=t_in.at[t_own(s)] if e == 0 else t_all.at[rows],
            dst_ref=t_all.at[rows],
            send_sem=tm_send.at[e, s],
            recv_sem=tm_recv.at[e, s],
            device_id=(pair, mate),
            device_id_type=MESH,
        )

    def landed(ref, rows, send, recv):
        pltpu.make_async_remote_copy(
            src_ref=ref.at[rows], dst_ref=ref.at[rows], send_sem=send, recv_sem=recv,
            device_id=(pair, mate), device_id_type=MESH,
        ).wait_recv()

    started = []

    def go(copy):
        copy.start()
        started.append(copy)

    for h in range(cuts):
        for to_right in (True, False):
            if carried(1, h, to_right):
                go(hop(1, h, to_right))
    for s in range(parts):
        for e in range(1, chips):
            go(t_cross(e, s))
    for s in range(parts):
        go(t_mate(0, s))
    own_b = pltpu.make_async_copy(
        b_in, b_all.at[pl.ds(pl.multiple_of(pair * rows_b, 8), rows_b)], local_sem.at[0]
    )
    own_t = pltpu.make_async_copy(
        t_in, t_all.at[pl.ds(pl.multiple_of(aux * rows_t * tiles, 8), rows_t * tiles)], local_sem.at[1]
    )
    own_b.start()
    own_t.start()
    own_b.wait()
    own_t.wait()

    def relay(d):
        for h in range(cuts):
            for from_left in (True, False):
                if carried(d, h, from_left):
                    arrive(d, h, from_left)
                    if d < reach and carried(d + 1, h, from_left):
                        go(hop(d + 1, h, from_left))

    def t_relay(s):
        for e in range(1, chips):
            landed(
                t_all, t_rows(chip_at(-e) * 2 + core, s),
                tx_send.at[e - 1, s], tx_recv.at[e - 1, s],
            )
            go(t_mate(e, s))

    def first_product(block):
        rows = pl.ds(pl.multiple_of(block * rows_b, 8), rows_b)
        high, low = split(b_all[rows, :])
        if rows_b % 16 == 0:
            b_high[pl.ds(pl.multiple_of(block * rows_b, 16), rows_b), :] = high.astype(BF16)
            b_low[pl.ds(pl.multiple_of(block * rows_b, 16), rows_b), :] = low.astype(BF16)
        both = jnp.concatenate([high, low], axis=0).astype(BF16)
        main = jnp.dot(both, t_high[...], preferred_element_type=F32)
        rest = jnp.dot(high.astype(BF16), t_low[...], preferred_element_type=F32)
        g_all[rows, :] = main[:rows_b] + (main[rows_b:] + rest)

    early = max(1, reach - 2)
    for d in range(1, early + 1):
        relay(d)
        for s in range(parts * (d - 1) // early, parts * d // early):
            t_relay(s)
    for e in range(chips):
        for s in range(parts):
            landed(
                t_all, t_rows(chip_at(-e) * 2 + (1 - core), s),
                tm_send.at[e, s], tm_recv.at[e, s],
            )

    @pl.loop(0, width // 128)
    def _(i):
        rows = pl.ds(pl.multiple_of(i * 128, 128), 128)
        for k in range(tiles):
            part = t_all[pl.ds(i * (128 * tiles) + k, 128, stride=tiles), :]
            high, low = split(part)
            t_high[rows, k * lanes:(k + 1) * lanes] = high.astype(BF16)
            t_low[rows, k * lanes:(k + 1) * lanes] = low.astype(BF16)

    @pl.loop(-(early - 1), early)
    def _(i):
        first_product(at(i))

    def both_sides(d):
        @pl.loop(0, 2)
        def _(i):
            first_product(at((2 * i - 1) * d))

    for d in range(early + 1, reach):
        relay(d)
        both_sides(d - 1)
    if reach > 1:
        both_sides(reach - 1)
    relay(reach)
    first_product(at(reach))

    if rows_b % 16:
        @pl.loop(0, width // 128)
        def _(i):
            rows = pl.ds(pl.multiple_of(i * 128, 128), 128)
            high, low = split(b_all[rows, :])
            b_high[rows, :] = high.astype(BF16)
            b_low[rows, :] = low.astype(BF16)

    def second_product(owner, s):
        high, low = split(g_all[g_rows(owner, s), :])
        both = jnp.concatenate([high, low], axis=0).astype(BF16)
        main = lax.dot_general(both, b_high[...], NT, preferred_element_type=F32)
        rest = lax.dot_general(high.astype(BF16), b_low[...], NT, preferred_element_type=F32)
        return main[:piece] + (main[piece:] + rest)

    def p_mate(e, s):
        return pltpu.make_async_remote_copy(
            src_ref=mate_out.at[e, s], dst_ref=mate_in.at[e, s],
            send_sem=pm_send.at[e, s], recv_sem=pm_recv.at[e, s],
            device_id=(pair, mate), device_id_type=MESH,
        )

    def p_cross(e, s):
        return pltpu.make_async_remote_copy(
            src_ref=sum_out.at[e - 1, s], dst_ref=sum_in.at[e - 1, s],
            send_sem=px_send.at[e - 1, s], recv_sem=px_recv.at[e - 1, s],
            device_id=(pair, chip_at(e) * 2 + core), device_id_type=MESH,
        )

    def chip_sum(e, s):
        mate_out[e, s] = second_product(chip_at(e) * 2 + (1 - core), s)
        p_mate(e, s).start()
        mine = second_product(chip_at(e) * 2 + core, s)
        p_mate(e, s).wait_recv()
        return mine + mate_in[e, s]

    @pl.loop(0, (chips - 1) * parts)
    def _(i):
        e, s = i // parts + 1, i % parts
        sum_out[e - 1, s] = chip_sum(e, s)
        p_cross(e, s).start()

    @pl.loop(0, parts)
    def _(s):
        kept[s] = chip_sum(0, s)

    for s in range(parts):
        total = kept[s]
        for e in range(1, chips):
            p_cross(e, s).wait_recv()
            total += sum_in[e - 1, s]
        for k in range(tiles):
            out[pl.ds(s * piece * tiles + k, piece, stride=tiles), :] = (
                total[:, k * lanes:(k + 1) * lanes]
            )

    for copy in started:
        copy.wait_send()
    for e in range(chips):
        for s in range(parts):
            p_mate(e, s).wait_send()
            if e:
                p_cross(e, s).wait_send()


def per_device(n, n_aux, amplitudes, fitting):
    rows_t, pair_dev, width = amplitudes.shape
    count_fit, rows_b, _ = fitting.shape
    assert pair_dev == 1 and count_fit == 1
    chips = n_aux // 2
    parts = PARTS if rows_t % (8 * PARTS) == 0 else 1
    piece = rows_t // parts
    cuts = CUTS
    reach = n // 2
    lanes = 128
    tiles = width // lanes
    dma = pltpu.SemaphoreType.DMA
    whole_f32 = pltpu.VMEM((width, width), F32)
    whole_bf16 = pltpu.VMEM((width, width), BF16)
    blocks = lambda k: pltpu.VMEM((k, parts, piece, width), F32)
    result = pl.pallas_call(
        functools.partial(kernel, n, chips, parts, cuts),
        out_shape=jax.ShapeDtypeStruct((rows_t * tiles, lanes), F32),
        in_specs=[pl.BlockSpec(memory_space=pl.ANY)] * 2,
        out_specs=pl.BlockSpec(memory_space=pltpu.VMEM),
        scratch_shapes=[
            pltpu.VMEM((width * tiles, lanes), F32), whole_f32, whole_bf16, whole_bf16, whole_bf16, whole_bf16, whole_f32,
            blocks(chips), blocks(chips), blocks(chips - 1), blocks(chips - 1),
            pltpu.VMEM((parts, piece, width), F32),
            dma((2,)),
            dma((reach, cuts)), dma((reach, cuts)), dma((reach, cuts)), dma((reach, cuts)),
            dma((chips - 1, parts)), dma((chips - 1, parts)),
            dma((chips, parts)), dma((chips, parts)),
            dma((chips, parts)), dma((chips, parts)),
            dma((chips - 1, parts)), dma((chips - 1, parts)),
        ],
        compiler_params=pltpu.CompilerParams(
            collective_id=0, has_side_effects=True, vmem_limit_bytes=60 << 20
        ),
    )(amplitudes.reshape(rows_t * tiles, lanes), fitting.reshape(rows_b, width))
    return result.reshape(rows_t, pair_dev, width)


def solution(mesh):
    spec = P("aux", "pair", None)
    return jax.shard_map(
        functools.partial(per_device, mesh.shape["pair"], mesh.shape["aux"]),
        mesh=mesh, in_specs=(spec, spec), out_specs=spec, check_vma=False,
    )
```

```python
import functools

import jax
import jax.numpy as jnp
from jax import lax
from jax.experimental import pallas as pl
from jax.experimental.pallas import tpu as pltpu
from jax.sharding import PartitionSpec as P

MESH = pl.DeviceIdType.MESH
CUTS, PARTS = 4, 4
F32, BF16 = jnp.float32, jnp.bfloat16
NT = (((1,), (1,)), ((), ()))


def ring_order(n):
    depth = 4 if n % 4 == 0 and n > 4 else 2
    width = n // depth
    if n % 2 or width < 2:
        return list(range(n))
    walk = []
    for z in range(depth):
        ys = range(1, width) if z % 2 == 0 else range(width - 1, 0, -1)
        walk += [z * width + y for y in ys]
    return walk + [z * width for z in range(depth - 1, -1, -1)]


def lookup(table, key):
    return sum(jnp.where(key == k, v, 0) for k, v in enumerate(table))


def split(v):
    high = v.astype(BF16).astype(F32)
    return high, v - high


def kernel(
    n, chips, parts, cuts,
    t_in, b_in, kept, received,
    t_all, b_all, t_high, t_low, b_high, b_low, g_all,
    mate_out, mate_in, sum_out, kept_v,
    local_sem, keep_sem, right_send, right_recv, left_send, left_recv,
    tx_send, tx_recv, tm_send, tm_recv, pm_send, pm_recv, px_send, px_recv,
):
    rows_b, width = b_in.shape
    lanes = t_in.shape[1]
    tiles = width // lanes
    rows_t = t_in.shape[0] // tiles
    piece = rows_t // parts
    reach = n // 2
    order = ring_order(n)
    where = [order.index(k) for k in range(n)]
    pair, aux = lax.axis_index("pair"), lax.axis_index("aux")
    chip, core = aux // 2, aux % 2
    mate = chip * 2 + (1 - core)
    spot = lookup(where, pair)

    def at(step):
        return lookup(order, lax.rem(spot + step + n, n))

    right, left = at(1), at(-1)

    def chip_at(step):
        return lax.rem(chip + step + chips, chips)

    barrier = pltpu.get_barrier_semaphore()
    greet = [(right, aux), (left, aux), (pair, mate)]
    greet += [(pair, chip_at(e) * 2 + core) for e in range(1, chips)]
    for who in greet:
        pl.semaphore_signal(barrier, inc=1, device_id=who, device_id_type=MESH)
    pl.semaphore_wait(barrier, len(greet))

    edges = [rows_b // 8 * k // cuts * 8 for k in range(cuts)] + [rows_b]
    bounds = [(a, b - a) for a, b in zip(edges, edges[1:])]

    def b_rows(block, h):
        start, size = bounds[h]
        return pl.ds(pl.multiple_of(block * rows_b + start, 8), size)

    def g_rows(owner, s):
        return pl.ds(pl.multiple_of(owner * rows_t + s * piece, 8), piece)

    def t_rows(owner, s):
        start = (owner * rows_t + s * piece) * tiles
        return pl.ds(pl.multiple_of(start, 8), piece * tiles)

    def t_own(s):
        return pl.ds(s * piece * tiles, piece * tiles)

    def hop(d, h, to_right):
        step = (1 - d) if to_right else (d - 1)
        block = at(step)
        rows = b_rows(block, h)
        start, size = bounds[h]
        src = b_in.at[pl.ds(start, size)] if d == 1 else b_all.at[rows]
        send, recv = (right_send, right_recv) if to_right else (left_send, left_recv)
        return pltpu.make_async_remote_copy(
            src_ref=src,
            dst_ref=b_all.at[rows],
            send_sem=send.at[d - 1, h],
            recv_sem=recv.at[d - 1, h],
            device_id=(right if to_right else left, aux),
            device_id_type=MESH,
        )

    def arrive(d, h, from_left):
        block = at(-d if from_left else d)
        rows = b_rows(block, h)
        send, recv = (right_send, right_recv) if from_left else (left_send, left_recv)
        pltpu.make_async_remote_copy(
            src_ref=b_all.at[rows],
            dst_ref=b_all.at[rows],
            send_sem=send.at[d - 1, h],
            recv_sem=recv.at[d - 1, h],
            device_id=(left if from_left else right, aux),
            device_id_type=MESH,
        ).wait_recv()

    def carried(d, h, to_right):
        return d < reach or (h < cuts // 2) == to_right

    def t_cross(e, s):
        return pltpu.make_async_remote_copy(
            src_ref=t_in.at[t_own(s)],
            dst_ref=t_all.at[t_rows(aux, s)],
            send_sem=tx_send.at[e - 1, s],
            recv_sem=tx_recv.at[e - 1, s],
            device_id=(pair, chip_at(e) * 2 + core),
            device_id_type=MESH,
        )

    def t_mate(e, s):
        rows = t_rows(chip_at(-e) * 2 + core, s)
        return pltpu.make_async_remote_copy(
            src_ref=t_in.at[t_own(s)] if e == 0 else t_all.at[rows],
            dst_ref=t_all.at[rows],
            send_sem=tm_send.at[e, s],
            recv_sem=tm_recv.at[e, s],
            device_id=(pair, mate),
            device_id_type=MESH,
        )

    def landed(ref, rows, send, recv):
        pltpu.make_async_remote_copy(
            src_ref=ref.at[rows], dst_ref=ref.at[rows], send_sem=send, recv_sem=recv,
            device_id=(pair, mate), device_id_type=MESH,
        ).wait_recv()

    started = []

    def go(copy):
        copy.start()
        started.append(copy)

    for h in range(cuts):
        for to_right in (True, False):
            if carried(1, h, to_right):
                go(hop(1, h, to_right))
    for s in range(parts):
        for e in range(1, chips):
            go(t_cross(e, s))
    for s in range(parts):
        go(t_mate(0, s))
    own_b = pltpu.make_async_copy(
        b_in, b_all.at[pl.ds(pl.multiple_of(pair * rows_b, 8), rows_b)], local_sem.at[0]
    )
    own_t = pltpu.make_async_copy(
        t_in, t_all.at[pl.ds(pl.multiple_of(aux * rows_t * tiles, 8), rows_t * tiles)], local_sem.at[1]
    )
    own_b.start()
    own_t.start()
    own_b.wait()
    own_t.wait()

    def relay(d):
        for h in range(cuts):
            for from_left in (True, False):
                if carried(d, h, from_left):
                    arrive(d, h, from_left)
                    if d < reach and carried(d + 1, h, from_left):
                        go(hop(d + 1, h, from_left))

    def t_relay(s):
        for e in range(1, chips):
            landed(
                t_all, t_rows(chip_at(-e) * 2 + core, s),
                tx_send.at[e - 1, s], tx_recv.at[e - 1, s],
            )
            go(t_mate(e, s))

    def first_product(block):
        rows = pl.ds(pl.multiple_of(block * rows_b, 8), rows_b)
        high, low = split(b_all[rows, :])
        if rows_b % 16 == 0:
            b_high[pl.ds(pl.multiple_of(block * rows_b, 16), rows_b), :] = high.astype(BF16)
            b_low[pl.ds(pl.multiple_of(block * rows_b, 16), rows_b), :] = low.astype(BF16)
        both = jnp.concatenate([high, low], axis=0).astype(BF16)
        main = jnp.dot(both, t_high[...], preferred_element_type=F32)
        rest = jnp.dot(high.astype(BF16), t_low[...], preferred_element_type=F32)
        g_all[rows, :] = main[:rows_b] + (main[rows_b:] + rest)

    early = max(1, reach - 2)
    for d in range(1, early + 1):
        relay(d)
        for s in range(parts * (d - 1) // early, parts * d // early):
            t_relay(s)
    for e in range(chips):
        for s in range(parts):
            landed(
                t_all, t_rows(chip_at(-e) * 2 + (1 - core), s),
                tm_send.at[e, s], tm_recv.at[e, s],
            )

    @pl.loop(0, width // 128)
    def _(i):
        rows = pl.ds(pl.multiple_of(i * 128, 128), 128)
        for k in range(tiles):
            part = t_all[pl.ds(i * (128 * tiles) + k, 128, stride=tiles), :]
            high, low = split(part)
            t_high[rows, k * lanes:(k + 1) * lanes] = high.astype(BF16)
            t_low[rows, k * lanes:(k + 1) * lanes] = low.astype(BF16)

    @pl.loop(-(early - 1), early)
    def _(i):
        first_product(at(i))

    def both_sides(d):
        @pl.loop(0, 2)
        def _(i):
            first_product(at((2 * i - 1) * d))

    for d in range(early + 1, reach):
        relay(d)
        both_sides(d - 1)
    if reach > 1:
        both_sides(reach - 1)
    relay(reach)
    first_product(at(reach))

    if rows_b % 16:
        @pl.loop(0, width // 128)
        def _(i):
            rows = pl.ds(pl.multiple_of(i * 128, 128), 128)
            high, low = split(b_all[rows, :])
            b_high[rows, :] = high.astype(BF16)
            b_low[rows, :] = low.astype(BF16)

    def second_product(owner, s):
        high, low = split(g_all[g_rows(owner, s), :])
        both = jnp.concatenate([high, low], axis=0).astype(BF16)
        main = lax.dot_general(both, b_high[...], NT, preferred_element_type=F32)
        rest = lax.dot_general(high.astype(BF16), b_low[...], NT, preferred_element_type=F32)
        return main[:piece] + (main[piece:] + rest)

    def p_mate(e, s):
        return pltpu.make_async_remote_copy(
            src_ref=mate_out.at[e, s], dst_ref=mate_in.at[e, s],
            send_sem=pm_send.at[e, s], recv_sem=pm_recv.at[e, s],
            device_id=(pair, mate), device_id_type=MESH,
        )

    def p_cross(e, s):
        return pltpu.make_async_remote_copy(
            src_ref=sum_out.at[e - 1, s], dst_ref=received.at[e - 1, s],
            send_sem=px_send.at[e - 1, s], recv_sem=px_recv.at[e - 1, s],
            device_id=(pair, chip_at(e) * 2 + core), device_id_type=MESH,
        )

    def keep(s):
        return pltpu.make_async_copy(kept_v.at[s], kept.at[s], keep_sem.at[s])

    def spread(ref, value):
        for k in range(tiles):
            ref[pl.ds(k, piece, stride=tiles), :] = value[:, k * lanes:(k + 1) * lanes]

    def chip_sum(e, s):
        mate_out[e, s] = second_product(chip_at(e) * 2 + (1 - core), s)
        p_mate(e, s).start()
        mine = second_product(chip_at(e) * 2 + core, s)
        p_mate(e, s).wait_recv()
        return mine + mate_in[e, s]

    @pl.loop(0, (chips - 1) * parts)
    def _(i):
        e, s = i // parts + 1, i % parts
        spread(sum_out.at[e - 1, s], chip_sum(e, s))
        p_cross(e, s).start()

    @pl.loop(0, parts)
    def _(s):
        spread(kept_v.at[s], chip_sum(0, s))
        keep(s).start()

    for s in range(parts):
        keep(s).wait()
        for e in range(1, chips):
            p_cross(e, s).wait_recv()

    for copy in started:
        copy.wait_send()
    for e in range(chips):
        for s in range(parts):
            p_mate(e, s).wait_send()
            if e:
                p_cross(e, s).wait_send()


def per_device(n, n_aux, amplitudes, fitting):
    rows_t, pair_dev, width = amplitudes.shape
    count_fit, rows_b, _ = fitting.shape
    assert pair_dev == 1 and count_fit == 1
    chips = n_aux // 2
    parts = PARTS if rows_t % (8 * PARTS) == 0 else 1
    piece = rows_t // parts
    cuts = CUTS
    reach = n // 2
    lanes = 128
    tiles = width // lanes
    dma = pltpu.SemaphoreType.DMA
    whole_f32 = pltpu.VMEM((width, width), F32)
    whole_bf16 = pltpu.VMEM((width, width), BF16)
    flat = (parts, piece * tiles, lanes)
    blocks = lambda k: pltpu.VMEM((k, parts, piece, width), F32)
    kept, received = pl.pallas_call(
        functools.partial(kernel, n, chips, parts, cuts),
        out_shape=[jax.ShapeDtypeStruct(flat, F32), jax.ShapeDtypeStruct((chips - 1,) + flat, F32)],
        in_specs=[pl.BlockSpec(memory_space=pl.ANY)] * 2,
        out_specs=[pl.BlockSpec(memory_space=pl.ANY)] * 2,
        scratch_shapes=[
            pltpu.VMEM((width * tiles, lanes), F32), whole_f32, whole_bf16, whole_bf16, whole_bf16, whole_bf16, whole_f32,
            blocks(chips), blocks(chips),
            pltpu.VMEM((chips - 1,) + flat, F32), pltpu.VMEM(flat, F32),
            dma((2,)), dma((parts,)),
            dma((reach, cuts)), dma((reach, cuts)), dma((reach, cuts)), dma((reach, cuts)),
            dma((chips - 1, parts)), dma((chips - 1, parts)),
            dma((chips, parts)), dma((chips, parts)),
            dma((chips, parts)), dma((chips, parts)),
            dma((chips - 1, parts)), dma((chips - 1, parts)),
        ],
        compiler_params=pltpu.CompilerParams(
            collective_id=0, has_side_effects=True, vmem_limit_bytes=60 << 20
        ),
    )(amplitudes.reshape(rows_t * tiles, lanes), fitting.reshape(rows_b, width))
    for e in range(chips - 1):
        kept = kept + received[e]
    return kept.reshape(rows_t, pair_dev, width)


def solution(mesh):
    spec = P("aux", "pair", None)
    return jax.shard_map(
        functools.partial(per_device, mesh.shape["pair"], mesh.shape["aux"]),
        mesh=mesh, in_specs=(spec, spec), out_specs=spec, check_vma=False,
    )
```

```python
import functools

import jax
import jax.numpy as jnp
from jax import lax
from jax.experimental import pallas as pl
from jax.experimental.pallas import tpu as pltpu
from jax.sharding import PartitionSpec as P

MESH = pl.DeviceIdType.MESH
CUTS, PARTS = 4, 4
F32, BF16 = jnp.float32, jnp.bfloat16
NT = (((1,), (1,)), ((), ()))


def ring_order(n):
    depth = 4 if n % 4 == 0 and n > 4 else 2
    width = n // depth
    if n % 2 or width < 2:
        return list(range(n))
    walk = []
    for z in range(depth):
        ys = range(1, width) if z % 2 == 0 else range(width - 1, 0, -1)
        walk += [z * width + y for y in ys]
    return walk + [z * width for z in range(depth - 1, -1, -1)]


def lookup(table, key):
    return sum(jnp.where(key == k, v, 0) for k, v in enumerate(table))


def split(v):
    high = v.astype(BF16).astype(F32)
    return high, v - high


def kernel(
    n, chips, parts, cuts,
    t_in, b_in, kept, received,
    t_all, b_all, t_high, t_low, b_high, b_low, g_all,
    mate_out, mate_in, sum_out, kept_v,
    local_sem, keep_sem, right_send, right_recv, left_send, left_recv,
    tx_send, tx_recv, tm_send, tm_recv, pm_send, pm_recv, px_send, px_recv,
):
    rows_b, width = b_in.shape
    lanes = t_in.shape[1]
    tiles = width // lanes
    rows_t = t_in.shape[0] // tiles
    piece = rows_t // parts
    reach = n // 2
    order = ring_order(n)
    where = [order.index(k) for k in range(n)]
    pair, aux = lax.axis_index("pair"), lax.axis_index("aux")
    chip, core = aux // 2, aux % 2
    mate = chip * 2 + (1 - core)
    spot = lookup(where, pair)

    def at(step):
        return lookup(order, lax.rem(spot + step + n, n))

    right, left = at(1), at(-1)

    def chip_at(step):
        return lax.rem(chip + step + chips, chips)

    barrier = pltpu.get_barrier_semaphore()
    greet = [(right, aux), (left, aux), (pair, mate)]
    greet += [(pair, chip_at(e) * 2 + core) for e in range(1, chips)]
    for who in greet:
        pl.semaphore_signal(barrier, inc=1, device_id=who, device_id_type=MESH)
    pl.semaphore_wait(barrier, len(greet))

    edges = [rows_b // 8 * k // cuts * 8 for k in range(cuts)] + [rows_b]
    bounds = [(a, b - a) for a, b in zip(edges, edges[1:])]

    def b_rows(block, h):
        start, size = bounds[h]
        return pl.ds(pl.multiple_of(block * rows_b + start, 8), size)

    def g_rows(owner, s):
        return pl.ds(pl.multiple_of(owner * rows_t + s * piece, 8), piece)

    def t_rows(owner, s):
        start = (owner * rows_t + s * piece) * tiles
        return pl.ds(pl.multiple_of(start, 8), piece * tiles)

    def t_own(s):
        return pl.ds(s * piece * tiles, piece * tiles)

    def hop(d, h, to_right):
        step = (1 - d) if to_right else (d - 1)
        block = at(step)
        rows = b_rows(block, h)
        start, size = bounds[h]
        src = b_in.at[pl.ds(start, size)] if d == 1 else b_all.at[rows]
        send, recv = (right_send, right_recv) if to_right else (left_send, left_recv)
        return pltpu.make_async_remote_copy(
            src_ref=src,
            dst_ref=b_all.at[rows],
            send_sem=send.at[d - 1, h],
            recv_sem=recv.at[d - 1, h],
            device_id=(right if to_right else left, aux),
            device_id_type=MESH,
        )

    def arrive(d, h, from_left):
        block = at(-d if from_left else d)
        rows = b_rows(block, h)
        send, recv = (right_send, right_recv) if from_left else (left_send, left_recv)
        pltpu.make_async_remote_copy(
            src_ref=b_all.at[rows],
            dst_ref=b_all.at[rows],
            send_sem=send.at[d - 1, h],
            recv_sem=recv.at[d - 1, h],
            device_id=(left if from_left else right, aux),
            device_id_type=MESH,
        ).wait_recv()

    def carried(d, h, to_right):
        return d < reach or (h < cuts // 2) == to_right

    def t_cross(e, s):
        return pltpu.make_async_remote_copy(
            src_ref=t_in.at[t_own(s)],
            dst_ref=t_all.at[t_rows(aux, s)],
            send_sem=tx_send.at[e - 1, s],
            recv_sem=tx_recv.at[e - 1, s],
            device_id=(pair, chip_at(e) * 2 + core),
            device_id_type=MESH,
        )

    def t_mate(e, s):
        rows = t_rows(chip_at(-e) * 2 + core, s)
        return pltpu.make_async_remote_copy(
            src_ref=t_in.at[t_own(s)] if e == 0 else t_all.at[rows],
            dst_ref=t_all.at[rows],
            send_sem=tm_send.at[e, s],
            recv_sem=tm_recv.at[e, s],
            device_id=(pair, mate),
            device_id_type=MESH,
        )

    def landed(ref, rows, send, recv):
        pltpu.make_async_remote_copy(
            src_ref=ref.at[rows], dst_ref=ref.at[rows], send_sem=send, recv_sem=recv,
            device_id=(pair, mate), device_id_type=MESH,
        ).wait_recv()

    started = []

    def go(copy):
        copy.start()
        started.append(copy)

    for h in range(cuts):
        for to_right in (True, False):
            if carried(1, h, to_right):
                go(hop(1, h, to_right))
    for s in range(parts):
        for e in range(1, chips):
            go(t_cross(e, s))
    for s in range(parts):
        go(t_mate(0, s))
    own_b = pltpu.make_async_copy(
        b_in, b_all.at[pl.ds(pl.multiple_of(pair * rows_b, 8), rows_b)], local_sem.at[0]
    )
    own_t = pltpu.make_async_copy(
        t_in, t_all.at[pl.ds(pl.multiple_of(aux * rows_t * tiles, 8), rows_t * tiles)], local_sem.at[1]
    )
    own_b.start()
    own_t.start()
    own_b.wait()
    own_t.wait()

    def relay(d):
        for h in range(cuts):
            for from_left in (True, False):
                if carried(d, h, from_left):
                    arrive(d, h, from_left)
                    if d < reach and carried(d + 1, h, from_left):
                        go(hop(d + 1, h, from_left))

    def t_relay(s):
        for e in range(1, chips):
            landed(
                t_all, t_rows(chip_at(-e) * 2 + core, s),
                tx_send.at[e - 1, s], tx_recv.at[e - 1, s],
            )
            go(t_mate(e, s))

    def first_product(block, late=False):
        rows = pl.ds(pl.multiple_of(block * rows_b, 8), rows_b)
        high, low = split(b_all[rows, :])
        if rows_b % 16 == 0 and not late:
            b_high[pl.ds(pl.multiple_of(block * rows_b, 16), rows_b), :] = high.astype(BF16)
            b_low[pl.ds(pl.multiple_of(block * rows_b, 16), rows_b), :] = low.astype(BF16)
        both = jnp.concatenate([high, low], axis=0).astype(BF16)
        main = jnp.dot(both, t_high[...], preferred_element_type=F32)
        rest = jnp.dot(high.astype(BF16), t_low[...], preferred_element_type=F32)
        g_all[rows, :] = main[:rows_b] + (main[rows_b:] + rest)

    early = max(1, reach - 2)
    for d in range(1, early + 1):
        relay(d)
        for s in range(parts * (d - 1) // early, parts * d // early):
            t_relay(s)
    for e in range(chips):
        for s in range(parts):
            landed(
                t_all, t_rows(chip_at(-e) * 2 + (1 - core), s),
                tm_send.at[e, s], tm_recv.at[e, s],
            )

    @pl.loop(0, width // 128)
    def _(i):
        rows = pl.ds(pl.multiple_of(i * 128, 128), 128)
        for k in range(tiles):
            part = t_all[pl.ds(i * (128 * tiles) + k, 128, stride=tiles), :]
            high, low = split(part)
            t_high[rows, k * lanes:(k + 1) * lanes] = high.astype(BF16)
            t_low[rows, k * lanes:(k + 1) * lanes] = low.astype(BF16)

    @pl.loop(-(early - 1), early)
    def _(i):
        first_product(at(i))

    def both_sides(d):
        @pl.loop(0, 2)
        def _(i):
            first_product(at((2 * i - 1) * d))

    for d in range(early + 1, reach):
        relay(d)
        both_sides(d - 1)
    if reach > 1:
        both_sides(reach - 1)
    relay(reach)
    far = at(reach)
    half = parts // 2 if rows_t == 2 * rows_b and rows_b % 16 == 0 and chips == 2 else 0
    if half:
        rows = pl.ds(pl.multiple_of(far * rows_b, 16), rows_b)
        high, low = split(b_all[pl.ds(pl.multiple_of(far * rows_b, 8), rows_b), :])
        b_high[rows, :] = high.astype(BF16)
        b_low[rows, :] = low.astype(BF16)
    else:
        first_product(far)

    if rows_b % 16:
        @pl.loop(0, width // 128)
        def _(i):
            rows = pl.ds(pl.multiple_of(i * 128, 128), 128)
            high, low = split(b_all[rows, :])
            b_high[rows, :] = high.astype(BF16)
            b_low[rows, :] = low.astype(BF16)

    def second_product(owner, s):
        high, low = split(g_all[g_rows(owner, s), :])
        both = jnp.concatenate([high, low], axis=0).astype(BF16)
        main = lax.dot_general(both, b_high[...], NT, preferred_element_type=F32)
        rest = lax.dot_general(high.astype(BF16), b_low[...], NT, preferred_element_type=F32)
        return main[:piece] + (main[piece:] + rest)

    def p_mate(e, s):
        return pltpu.make_async_remote_copy(
            src_ref=mate_out.at[e, s], dst_ref=mate_in.at[e, s],
            send_sem=pm_send.at[e, s], recv_sem=pm_recv.at[e, s],
            device_id=(pair, mate), device_id_type=MESH,
        )

    def p_cross(e, s):
        return pltpu.make_async_remote_copy(
            src_ref=sum_out.at[e - 1, s], dst_ref=received.at[e - 1, s],
            send_sem=px_send.at[e - 1, s], recv_sem=px_recv.at[e - 1, s],
            device_id=(pair, chip_at(e) * 2 + core), device_id_type=MESH,
        )

    def keep(s):
        return pltpu.make_async_copy(kept_v.at[s], kept.at[s], keep_sem.at[s])

    def spread(ref, value):
        for k in range(tiles):
            ref[pl.ds(k, piece, stride=tiles), :] = value[:, k * lanes:(k + 1) * lanes]

    def chip_sum(e, s):
        mate_out[e, s] = second_product(chip_at(e) * 2 + (1 - core), s)
        p_mate(e, s).start()
        mine = second_product(chip_at(e) * 2 + core, s)
        p_mate(e, s).wait_recv()
        return mine + mate_in[e, s]

    def cross(i):
        e, s = i // parts + 1, lax.rem(i + half * (1 - far % 2), parts)
        spread(sum_out.at[e - 1, s], chip_sum(e, s))
        p_cross(e, s).start()

    if half:
        @pl.loop(0, half)
        def _(i):
            cross(i)

        first_product(far, late=True)

    @pl.loop(half, (chips - 1) * parts)
    def _(i):
        cross(i)

    @pl.loop(0, parts)
    def _(s):
        spread(kept_v.at[s], chip_sum(0, s))
        keep(s).start()

    for s in range(parts):
        keep(s).wait()
        for e in range(1, chips):
            p_cross(e, s).wait_recv()

    for copy in started:
        copy.wait_send()
    for e in range(chips):
        for s in range(parts):
            p_mate(e, s).wait_send()
            if e:
                p_cross(e, s).wait_send()


def per_device(n, n_aux, amplitudes, fitting):
    rows_t, pair_dev, width = amplitudes.shape
    count_fit, rows_b, _ = fitting.shape
    assert pair_dev == 1 and count_fit == 1
    chips = n_aux // 2
    parts = PARTS if rows_t % (8 * PARTS) == 0 else 1
    piece = rows_t // parts
    cuts = CUTS
    reach = n // 2
    lanes = 128
    tiles = width // lanes
    dma = pltpu.SemaphoreType.DMA
    whole_f32 = pltpu.VMEM((width, width), F32)
    whole_bf16 = pltpu.VMEM((width, width), BF16)
    flat = (parts, piece * tiles, lanes)
    blocks = lambda k: pltpu.VMEM((k, parts, piece, width), F32)
    kept, received = pl.pallas_call(
        functools.partial(kernel, n, chips, parts, cuts),
        out_shape=[jax.ShapeDtypeStruct(flat, F32), jax.ShapeDtypeStruct((chips - 1,) + flat, F32)],
        in_specs=[pl.BlockSpec(memory_space=pl.ANY)] * 2,
        out_specs=[pl.BlockSpec(memory_space=pl.ANY)] * 2,
        scratch_shapes=[
            pltpu.VMEM((width * tiles, lanes), F32), whole_f32, whole_bf16, whole_bf16, whole_bf16, whole_bf16, whole_f32,
            blocks(chips), blocks(chips),
            pltpu.VMEM((chips - 1,) + flat, F32), pltpu.VMEM(flat, F32),
            dma((2,)), dma((parts,)),
            dma((reach, cuts)), dma((reach, cuts)), dma((reach, cuts)), dma((reach, cuts)),
            dma((chips - 1, parts)), dma((chips - 1, parts)),
            dma((chips, parts)), dma((chips, parts)),
            dma((chips, parts)), dma((chips, parts)),
            dma((chips - 1, parts)), dma((chips - 1, parts)),
        ],
        compiler_params=pltpu.CompilerParams(
            collective_id=0, has_side_effects=True, vmem_limit_bytes=60 << 20
        ),
    )(amplitudes.reshape(rows_t * tiles, lanes), fitting.reshape(rows_b, width))
    for e in range(chips - 1):
        kept = kept + received[e]
    return kept.reshape(rows_t, pair_dev, width)


def solution(mesh):
    spec = P("aux", "pair", None)
    return jax.shard_map(
        functools.partial(per_device, mesh.shape["pair"], mesh.shape["aux"]),
        mesh=mesh, in_specs=(spec, spec), out_specs=spec, check_vma=False,
    )
```
